32 devices in a mesh: grp: 2 (over y), loan: 4 (over z), feat: 4 (over x, core).
Axes of the slice: x: 2, y: 2, z: 4, core: 2. Of those that a mesh axis runs over, the one named last changes fastest.
Arguments:
- design: bfloat16 [16384, 4096], P(('grp', 'loan'), 'feat'), parts along dimension 0, may hold values from -6 to 6
- labels: int32 [16384], P(('grp', 'loan')), parts along dimension 0, may hold values from 0 to 1
- pool_ids: int32 [16384], P(('grp', 'loan')), parts along dimension 0, may hold values from 0 to 255, as said below
- pool_region_index: int32 [512], P(('grp', 'loan')), parts along dimension 0, may hold values from 0 to 63
- step_size: float32 [32], P('grp'), parts along dimension 0, may hold values from 0.005 to 0.02
- beta: float32 [32, 4096], P('grp', 'feat'), parts along dimension 0, may hold values from -0.09375 to 0.09375
- pools: float32 [32, 256, 256], P('grp', 'loan', 'feat'), parts along dimension 0, may hold values from -0.5 to 0.5
- regions: float32 [32, 64, 256], P('grp', None, 'feat'), parts along dimension 0, may hold values from -0.5 to 0.5
- beta_momentum: float32 [32, 4096], P('grp', 'feat'), parts along dimension 0, may hold values from -6 to 6
- pool_momentum: float32 [32, 256, 256], P('grp', 'loan', 'feat'), parts along dimension 0, may hold values from -6 to 6
- region_momentum: float32 [32, 64, 256], P('grp', None, 'feat'), parts along dimension 0, may hold values from -6 to 6
Outputs:
- beta_next: float32 [32, 4096], P('grp', 'feat'), parts along dimension 0
- pools_next: float32 [32, 256, 256], P('grp', 'loan', 'feat'), parts along dimension 0
- regions_next: float32 [32, 64, 256], P('grp', None, 'feat'), parts along dimension 0
- beta_momentum_next: float32 [32, 4096], P('grp', 'feat'), parts along dimension 0
- pool_momentum_next: float32 [32, 256, 256], P('grp', 'loan', 'feat'), parts along dimension 0
- region_momentum_next: float32 [32, 64, 256], P('grp', None, 'feat'), parts along dimension 0
The draws below stay inside these ranges and needn't reach their ends.
There are 2 independent parts, one for each index of `grp`. The reference program is written for one: setup_inputs(seed, part) draws one part's arguments, and reference() takes and returns one part's arrays. A program takes and returns all parts, laid end to end along the dimension named above; each array names one. Nothing has to cross between parts.
Inputs may be any that keep to these rules, and one draw needn't show every extreme that they name: `pool_ids`: in each aligned block of 2048 loans (block l counted from 0) the pool ids lie in l * 64 to (l + 1) * 64 - 1 and do not fall along the block.
All inputs are finite; a program needn't handle non-finite values.
Results may differ from the reference program's by a relative error of at most 0.0006.
Values may be sent and summed in bfloat16 or wider, within the bound.
A program may use at most 64 MiB of HBM per device.

```python
import math
import jax
import jax.numpy as jnp
from jax import lax

F = 4096
G = 256
R = 64
CHAINS = 16
ROWS_DEV = 2048
POOLS_DEV = 64
LOANS = 8192
POOLS = 256
N_LOAN = 4


def draw_pool_ids(key, part):
    blocks = jax.random.randint(key, (N_LOAN, ROWS_DEV), 0, POOLS_DEV)
    blocks = jnp.sort(blocks, axis=1) + jnp.arange(N_LOAN, dtype=jnp.int32)[:, None] * POOLS_DEV
    return blocks.reshape(-1).astype(jnp.int32)


def plant(entries, stream_key, low, high):
    index_at = [jax.random.randint(jax.random.fold_in(stream_key, axis), (), 0, length) for axis, length in enumerate(entries.shape)]
    longest = entries.shape.index(max(entries.shape))
    beside = index_at[:longest] + [(index_at[longest] + 1) % entries.shape[longest]] + index_at[longest + 1:]
    return entries.at[tuple(index_at)].set(low).at[tuple(beside)].set(high)


def steps_of(key, shape, pieces, low, top_value):
    level, own = 1.0, jax.random.fold_in(key, 6)
    for axis_at, blocks in pieces:
        draws = jnp.exp(jax.random.uniform(jax.random.fold_in(own, axis_at), (blocks,), jnp.float32, low / len(pieces), top_value / len(pieces)))
        level = level * jnp.repeat(draws, shape[axis_at] // blocks).reshape([-1 if axis == axis_at else 1 for axis in range(len(shape))])
    return level


def noise(rng, dims, spread, bound, cuts=(), kind=jnp.bfloat16):
    factor_of = steps_of(rng, dims, cuts, -0.22, 0.18) if cuts else 1.0
    drawn = jax.random.normal(rng, dims, jnp.float32) * spread * factor_of
    return jnp.minimum(jnp.maximum(drawn, -bound), bound).astype(kind)


def setup_inputs(seed: int = 0, part: int = 0) -> dict:
    key_of = jax.random.split(jax.random.key(seed), 12)
    part_splits = jax.random.split(jax.random.fold_in(key_of[11], part), 12)
    return {
        "design": noise(part_splits[0], (LOANS, F), 1.0, 6.0, ((0, 4), (1, 4))),
        "labels": plant(jax.random.randint(part_splits[1], (LOANS,), 0, 2), jax.random.fold_in(part_splits[1], 1), 0, 1).astype(jnp.int32),
        "pool_ids": draw_pool_ids(jax.random.fold_in(jax.random.fold_in(key_of[11], part), 71), part),
        "pool_region_index": plant(jax.random.randint(part_splits[3], (POOLS,), 0, R), jax.random.fold_in(part_splits[3], 1), 0, R - 1).astype(jnp.int32),
        "step_size": jnp.clip(jnp.exp(jax.random.uniform(part_splits[4], (CHAINS,), jnp.float32, math.log(0.005), math.log(0.02))), 0.005, 0.02),
        "beta": noise(part_splits[5], (CHAINS, F), F ** -0.5, 0.09375, ((1, 4),), jnp.float32),
        "pools": noise(part_splits[6], (CHAINS, POOLS, G), 0.0625, 0.5, ((1, 4), (2, 4)), jnp.float32),
        "regions": noise(part_splits[7], (CHAINS, R, G), 0.0625, 0.5, ((2, 4),), jnp.float32),
        "beta_momentum": noise(part_splits[8], (CHAINS, F), 1.0, 6.0, ((1, 4),), jnp.float32),
        "pool_momentum": noise(part_splits[9], (CHAINS, POOLS, G), 1.0, 6.0, ((1, 4), (2, 4)), jnp.float32),
        "region_momentum": noise(part_splits[10], (CHAINS, R, G), 1.0, 6.0, ((2, 4),), jnp.float32),
    }


MATMUL_ACCURACY = 256.0


def gradient(design, labels, pool_ids, pool_region_index, b, upper_operand, lower_operand):
    stride = F // G
    slope_feats = design[:, ::stride].astype(jnp.float32)
    b16 = b.astype(jnp.bfloat16)
    linear = lax.dot_general(b16, design, (((1,), (1,)), ((), ())), preferred_element_type=jnp.float32)
    term = lax.map(lambda uc: jnp.sum(slope_feats * uc[pool_ids], axis=1), upper_operand)
    logit = linear + term
    resid = (labels.astype(jnp.float32)[None, :] - jax.nn.sigmoid(logit)).astype(jnp.bfloat16)
    xt = lax.dot_general(resid, design, (((1,), (0,)), ((), ())), preferred_element_type=jnp.float32)
    gb = xt - F * b
    rf = resid.astype(jnp.float32)
    lik = lax.map(lambda rc: jax.ops.segment_sum(slope_feats * rc[:, None], pool_ids, num_segments=POOLS), rf)
    selected_operand = lower_operand[:, pool_region_index, :]
    device_index = MATMUL_ACCURACY * (upper_operand - selected_operand)
    gu = lik - device_index
    sums = jax.ops.segment_sum(jnp.moveaxis(device_index, 1, 0), pool_region_index, num_segments=R)
    gv = jnp.moveaxis(sums, 0, 1) - MATMUL_ACCURACY * lower_operand
    return gb, gu, gv


def reference(design, labels, pool_ids, pool_region_index, step_size, beta, pools, regions, beta_momentum, pool_momentum, region_momentum):
    half = 0.5 * step_size
    h2 = half[:, None]
    h3 = half[:, None, None]
    e2 = step_size[:, None]
    e3 = step_size[:, None, None]
    gb, gu, gv = gradient(design, labels, pool_ids, pool_region_index, beta, pools, regions)
    mb = beta_momentum + h2 * gb
    mu = pool_momentum + h3 * gu
    mv = region_momentum + h3 * gv
    beta_next = beta + e2 * mb
    pools_next = pools + e3 * mu
    regions_next = regions + e3 * mv
    gb, gu, gv = gradient(design, labels, pool_ids, pool_region_index, beta_next, pools_next, regions_next)
    return beta_next, pools_next, regions_next, mb + h2 * gb, mu + h3 * gu, mv + h3 * gv
```

```python
import functools

import jax
import jax.numpy as jnp
from jax import lax
from jax.experimental import pallas as pl
from jax.experimental.pallas import tpu as pltpu
from jax.sharding import PartitionSpec as P

PREC = 256.0
MESH = pl.DeviceIdType.MESH
NT = (((1,), (1,)), ((), ()))
NN = (((1,), (0,)), ((), ()))
F32 = jnp.float32
BF16 = jnp.bfloat16


def dot(a, b, dims=NN):
    return lax.dot_general(a, b, dims, preferred_element_type=F32)


def split3(x):
    hi = x.astype(BF16)
    rest = x - hi.astype(F32)
    mid = rest.astype(BF16)
    lo = (rest - mid.astype(F32)).astype(BF16)
    return jnp.concatenate([hi, mid, lo], axis=0)


def kernel(
    nf,
    nl,
    design,
    labels,
    ids,
    pri_col,
    pri_row,
    step_s,
    step_col,
    beta,
    pools,
    regions,
    beta_m,
    pool_m,
    region_m,
    beta_n,
    pools_n,
    regions_n,
    beta_mn,
    pool_mn,
    region_mn,
    mask,
    slope_t,
    slope,
    u2,
    dev,
    lik,
    term,
    part,
    rs_buf,
    resid,
    resid_f,
    xt_buf,
    reg_part,
    reg_buf,
    reg_own,
    reg_all,
    s_rs,
    r_rs,
    s_ag,
    r_ag,
    s_xt,
    r_xt,
    s_rr,
    r_rr,
    s_ra,
    r_ra,
):
    fi = lax.axis_index("feat")
    li = lax.axis_index("loan")
    chains = beta.shape[0]
    feats = design.shape[1]
    owned = pools.shape[1]
    g_own = pools.shape[2]
    n_reg = regions.shape[1]
    width = labels.shape[2]
    per = chains // nl
    stride = feats // g_own
    total_feats = float(feats * nf)

    def at(axis, n, i, k):
        return lax.rem(i + k, n)

    barrier = pltpu.get_barrier_semaphore()
    for k in range(1, nf):
        pl.semaphore_signal(
            barrier, inc=1, device_id={"feat": at("feat", nf, fi, k)}, device_id_type=MESH
        )
    for k in range(1, nl):
        pl.semaphore_signal(
            barrier, inc=1, device_id={"loan": at("loan", nl, li, k)}, device_id_type=MESH
        )

    def rows(j):
        return design[pl.ds(pl.multiple_of(j * width, width), width), :]

    def remote(src, dst, ss, rs, axis, peer):
        return pltpu.make_async_remote_copy(
            src_ref=src,
            dst_ref=dst,
            send_sem=ss,
            recv_sem=rs,
            device_id={axis: peer},
            device_id_type=MESH,
        )

    def rs_copy(t, k):
        peer = lax.rem(fi + k, nf)
        return remote(
            part.at[t, peer], rs_buf.at[t, k - 1], s_rs.at[t, k - 1], r_rs.at[t, k - 1], "feat", peer
        )

    def ag_copy(t, k, slot):
        peer = lax.rem(fi + k, nf)
        return remote(
            resid.at[t, slot], resid.at[t, slot], s_ag.at[t, k - 1], r_ag.at[t, k - 1], "feat", peer
        )

    def xt_copy(t, k):
        peer = lax.rem(li + k, nl)
        return remote(
            xt_buf.at[t, 0], xt_buf.at[t, k], s_xt.at[t, k - 1], r_xt.at[t, k - 1], "loan", peer
        )

    def rr_copy(t, k):
        peer = lax.rem(li + k, nl)
        return remote(
            reg_part.at[t, pl.ds(peer * per, per)],
            reg_buf.at[t, k - 1],
            s_rr.at[t, k - 1],
            r_rr.at[t, k - 1],
            "loan",
            peer,
        )

    def ra_copy(t, k, owner):
        peer = lax.rem(li + k, nl)
        return remote(
            reg_own.at[t],
            reg_all.at[t, owner],
            s_ra.at[t, k - 1],
            r_ra.at[t, k - 1],
            "loan",
            peer,
        )

    oh = (pri_col[...] == lax.broadcasted_iota(jnp.int32, (owned, n_reg), 1)).astype(F32)
    oh3 = jnp.concatenate([oh, oh, oh], axis=1).astype(BF16)
    oht = (pri_row[...] == lax.broadcasted_iota(jnp.int32, (n_reg, owned), 0)).astype(F32)
    oht3 = jnp.concatenate([oht, oht, oht], axis=1).astype(BF16)

    def region_dev(t, u_ref, v_ref):
        for c in range(chains):
            d = PREC * (u_ref[c] - dot(oh3, split3(v_ref[c])))
            dev[c] = d
            reg_part[t, c] = dot(oht3, split3(d))
        for k in range(1, nl):
            rr_copy(t, k).start()

    def region_reduce(t):
        for k in range(1, nl):
            rr_copy(t, k).wait_recv()
        total = reg_part[t, pl.ds(li * per, per)]
        for k in range(1, nl):
            total = total + reg_buf[t, k - 1]
        reg_own[t] = total
        for k in range(1, nl):
            ra_copy(t, k, li).start()
        reg_all[t, li] = total

    def region_gather(t):
        for k in range(1, nl):
            ra_copy(t, k, lax.rem(li + nl - k, nl)).wait_recv()

    def pool_terms(u_ref):
        for c in range(chains):
            u = u_ref[c]
            hi = u.astype(BF16).astype(F32)
            both = jnp.concatenate([hi, u - hi], axis=1)
            u2[pl.ds(c * owned, owned), :] = both.astype(BF16)

        def chunk(j, carry):
            z = dot(u2[...], slope_t[j])
            m = mask[j]
            for c in range(chains):
                term[j, pl.ds(c, 1), :] = jnp.sum(
                    z[c * owned : (c + 1) * owned] * m, axis=0, keepdims=True
                )
            return carry

        lax.fori_loop(0, nf, chunk, 0)

    def logits(t, b_ref):
        b16 = b_ref[...].astype(BF16)

        def chunk(j, carry):
            part[t, j] = term[j] + dot(b16, rows(j), NT)
            return carry

        lax.fori_loop(0, nf, chunk, 0)
        for k in range(1, nf):
            rs_copy(t, k).start()

    def residuals(t):
        for k in range(1, nf):
            rs_copy(t, k).wait_recv()
        logit = part[t, fi]
        for k in range(1, nf):
            logit = logit + rs_buf[t, k - 1]
        mine = (labels[fi].astype(F32) - jax.nn.sigmoid(logit)).astype(BF16)
        resid[t, fi] = mine
        for k in range(1, nf):
            ag_copy(t, k, fi).start()

    def population(t):
        total = dot(resid[t, fi], rows(fi))
        for k in range(1, nf):
            source = lax.rem(fi + nf - k, nf)
            ag_copy(t, k, source).wait_recv()
            total = total + dot(resid[t, source], rows(source))
        xt_buf[t, 0] = total
        for k in range(1, nl):
            xt_copy(t, k).start()

    def population_sum(t):
        for k in range(1, nl):
            xt_copy(t, k).wait_recv()
        total = xt_buf[t, li]
        for j in range(1, nl):
            total = total + xt_buf[t, lax.rem(li + nl - j, nl)]
        return total

    def likelihood(t):
        resid_f[...] = resid[t].astype(F32)
        lik[...] = jnp.zeros_like(lik)

        def chunk(j, carry):
            m = mask[j]
            a = jnp.concatenate(
                [(resid_f[j, pl.ds(c, 1), :] * m).astype(BF16) for c in range(chains)], axis=0
            )
            lik[...] += dot(a, slope[j])
            return carry

        lax.fori_loop(0, nf, chunk, 0)

    pick_t = (
        lax.broadcasted_iota(jnp.int32, (g_own, feats), 1)
        == stride * lax.broadcasted_iota(jnp.int32, (g_own, feats), 0)
    ).astype(F32).astype(BF16)
    first = li * owned

    def prepare(j, carry):
        x = rows(j)
        st = dot(pick_t, x, NT).astype(BF16)
        slope_t[j] = jnp.concatenate([st, st], axis=0)
        slope[j] = dot(x, pick_t, NT).astype(BF16)
        mask[j] = (
            ids[j] - first == lax.broadcasted_iota(jnp.int32, (owned, width), 0)
        ).astype(F32)
        return carry

    lax.fori_loop(0, nf, prepare, 0)
    half = 0.5 * step_col[...]

    pool_terms(pools)
    pl.semaphore_wait(barrier, nf + nl - 2)
    logits(0, beta)
    region_dev(0, pools, regions)
    residuals(0)
    region_reduce(0)
    population(0)
    likelihood(0)
    for c in range(chains):
        e = step_s[c]
        m = pool_m[c] + (0.5 * e) * (lik[pl.ds(c * owned, owned), :] - dev[c])
        pool_mn[c] = m
        pools_n[c] = pools[c] + e * m
    region_gather(0)
    for c in range(chains):
        e = step_s[c]
        g = reg_all[0, c // per, c % per] - PREC * regions[c]
        m = region_m[c] + (0.5 * e) * g
        region_mn[c] = m
        regions_n[c] = regions[c] + e * m
    region_dev(1, pools_n, regions_n)
    pool_terms(pools_n)
    mb = beta_m[...] + half * (population_sum(0) - total_feats * beta[...])
    beta_mn[...] = mb
    beta_n[...] = beta[...] + step_col[...] * mb
    logits(1, beta_n)
    region_reduce(1)
    residuals(1)
    population(1)
    likelihood(1)
    for c in range(chains):
        pool_mn[c] = pool_mn[c] + (0.5 * step_s[c]) * (lik[pl.ds(c * owned, owned), :] - dev[c])
    region_gather(1)
    for c in range(chains):
        g = reg_all[1, c // per, c % per] - PREC * regions_n[c]
        region_mn[c] = region_mn[c] + (0.5 * step_s[c]) * g
    beta_mn[...] = beta_mn[...] + half * (population_sum(1) - total_feats * beta_n[...])
    for t in range(2):
        for k in range(1, nf):
            rs_copy(t, k).wait_send()
            ag_copy(t, k, fi).wait_send()
        for k in range(1, nl):
            xt_copy(t, k).wait_send()
            rr_copy(t, k).wait_send()
            ra_copy(t, k, li).wait_send()


def body(
    nf,
    nl,
    design,
    labels,
    pool_ids,
    pool_region_index,
    step_size,
    beta,
    pools,
    regions,
    beta_momentum,
    pool_momentum,
    region_momentum,
):
    loans, feats = design.shape
    chains, owned, g_own = pools.shape
    n_reg = regions.shape[1]
    width = loans // nf
    per = chains // nl
    vmem = pl.BlockSpec(memory_space=pltpu.VMEM)
    smem = pl.BlockSpec(memory_space=pltpu.SMEM)
    dma = pltpu.SemaphoreType.DMA
    args = (
        design,
        labels.reshape(nf, 1, width),
        pool_ids.reshape(nf, 1, width),
        pool_region_index.reshape(owned, 1),
        pool_region_index.reshape(1, owned),
        step_size,
        step_size.reshape(chains, 1),
        beta,
        pools,
        regions,
        beta_momentum,
        pool_momentum,
        region_momentum,
    )
    outs = (beta, pools, regions, beta_momentum, pool_momentum, region_momentum)
    return pl.pallas_call(
        functools.partial(kernel, nf, nl),
        out_shape=tuple(jax.ShapeDtypeStruct(x.shape, x.dtype) for x in outs),
        in_specs=[smem if i == 5 else vmem for i in range(len(args))],
        out_specs=tuple(vmem for _ in outs),
        scratch_shapes=[
            pltpu.VMEM((nf, owned, width), F32),
            pltpu.VMEM((nf, 2 * g_own, width), BF16),
            pltpu.VMEM((nf, width, g_own), BF16),
            pltpu.VMEM((chains * owned, 2 * g_own), BF16),
            pltpu.VMEM((chains, owned, g_own), F32),
            pltpu.VMEM((chains * owned, g_own), F32),
            pltpu.VMEM((nf, chains, width), F32),
            pltpu.VMEM((2, nf, chains, width), F32),
            pltpu.VMEM((2, nf - 1, chains, width), F32),
            pltpu.VMEM((2, nf, chains, width), BF16),
            pltpu.VMEM((nf, chains, width), F32),
            pltpu.VMEM((2, nl, chains, feats), F32),
            pltpu.VMEM((2, chains, n_reg, g_own), F32),
            pltpu.VMEM((2, nl - 1, per, n_reg, g_own), F32),
            pltpu.VMEM((2, per, n_reg, g_own), F32),
            pltpu.VMEM((2, nl, per, n_reg, g_own), F32),
            dma((2, nf - 1)),
            dma((2, nf - 1)),
            dma((2, nf - 1)),
            dma((2, nf - 1)),
            dma((2, nl - 1)),
            dma((2, nl - 1)),
            dma((2, nl - 1)),
            dma((2, nl - 1)),
            dma((2, nl - 1)),
            dma((2, nl - 1)),
        ],
        compiler_params=pltpu.CompilerParams(
            collective_id=0, has_side_effects=True, vmem_limit_bytes=60 << 20
        ),
    )(*args)


def solution(mesh):
    in_specs = (
        P(("grp", "loan"), "feat"),
        P(("grp", "loan")),
        P(("grp", "loan")),
        P(("grp", "loan")),
        P("grp"),
        P("grp", "feat"),
        P("grp", "loan", "feat"),
        P("grp", None, "feat"),
        P("grp", "feat"),
        P("grp", "loan", "feat"),
        P("grp", None, "feat"),
    )
    out_specs = (
        P("grp", "feat"),
        P("grp", "loan", "feat"),
        P("grp", None, "feat"),
        P("grp", "feat"),
        P("grp", "loan", "feat"),
        P("grp", None, "feat"),
    )
    step = functools.partial(body, mesh.shape["feat"], mesh.shape["loan"])
    return jax.shard_map(step, mesh=mesh, in_specs=in_specs, out_specs=out_specs, check_vma=False)
```

```python
import functools

import jax
import jax.numpy as jnp
from jax import lax
from jax.experimental import pallas as pl
from jax.experimental.pallas import tpu as pltpu
from jax.sharding import PartitionSpec as P

PREC = 256.0
MESH = pl.DeviceIdType.MESH
NT = (((1,), (1,)), ((), ()))
NN = (((1,), (0,)), ((), ()))
F32 = jnp.float32
BF16 = jnp.bfloat16


def dot(a, b, dims=NN):
    return lax.dot_general(a, b, dims, preferred_element_type=F32)


def split3(x):
    hi = x.astype(BF16)
    rest = x - hi.astype(F32)
    mid = rest.astype(BF16)
    lo = (rest - mid.astype(F32)).astype(BF16)
    return jnp.concatenate([hi, mid, lo], axis=0)


def kernel(
    nf,
    nl,
    design_hbm,
    labels,
    ids,
    pri_row,
    step_s,
    beta,
    pools,
    regions,
    beta_m,
    pool_m,
    region_m,
    beta_n,
    pools_n,
    regions_n,
    beta_mn,
    pool_mn,
    region_mn,
    design,
    mask,
    slope_t,
    slope,
    u2,
    dev,
    lik,
    term,
    part,
    rs_buf,
    resid,
    resid_f,
    xt_buf,
    reg_part,
    reg_buf,
    reg_own,
    reg_all,
    load,
    s_rs,
    r_rs,
    s_ag,
    r_ag,
    s_xt,
    r_xt,
    s_rr,
    r_rr,
    s_ra,
    r_ra,
):
    fi = lax.axis_index("feat")
    li = lax.axis_index("loan")
    chains = beta.shape[0]
    feats = design.shape[1]
    owned = pools.shape[1]
    g_own = pools.shape[2]
    n_reg = regions.shape[1]
    width = labels.shape[2]
    per = chains // nl
    stride = feats // g_own
    total_feats = float(feats * nf)

    def at(axis, n, i, k):
        return lax.rem(i + k, n)

    fetch = pltpu.make_async_copy(design_hbm, design, load)
    fetch.start()
    fold = folds(n_reg, g_own)
    lines = n_reg // fold

    def pack(x):
        return jnp.concatenate([x[i * lines : (i + 1) * lines] for i in range(fold)], axis=1)

    def unpack(x):
        return jnp.concatenate([x[:, i * g_own : (i + 1) * g_own] for i in range(fold)], axis=0)

    barrier = pltpu.get_barrier_semaphore()
    for k in range(1, nf):
        pl.semaphore_signal(
            barrier, inc=1, device_id={"feat": at("feat", nf, fi, k)}, device_id_type=MESH
        )
    for k in range(1, nl):
        pl.semaphore_signal(
            barrier, inc=1, device_id={"loan": at("loan", nl, li, k)}, device_id_type=MESH
        )

    def rows(j):
        return design[pl.ds(pl.multiple_of(j * width, width), width), :]

    def remote(src, dst, ss, rs, axis, peer):
        return pltpu.make_async_remote_copy(
            src_ref=src,
            dst_ref=dst,
            send_sem=ss,
            recv_sem=rs,
            device_id={axis: peer},
            device_id_type=MESH,
        )

    def rs_copy(t, k):
        peer = lax.rem(fi + k, nf)
        return remote(
            part.at[t, peer], rs_buf.at[t, k - 1], s_rs.at[t, k - 1], r_rs.at[t, k - 1], "feat", peer
        )

    def ag_copy(t, k, slot):
        peer = lax.rem(fi + k, nf)
        return remote(
            resid.at[t, slot], resid.at[t, slot], s_ag.at[t, k - 1], r_ag.at[t, k - 1], "feat", peer
        )

    def xt_copy(t, k):
        peer = lax.rem(li + k, nl)
        return remote(
            xt_buf.at[t, 0], xt_buf.at[t, k], s_xt.at[t, k - 1], r_xt.at[t, k - 1], "loan", peer
        )

    def rr_copy(t, k):
        peer = lax.rem(li + k, nl)
        return remote(
            reg_part.at[t, pl.ds(peer * per, per)],
            reg_buf.at[t, k - 1],
            s_rr.at[t, k - 1],
            r_rr.at[t, k - 1],
            "loan",
            peer,
        )

    def ra_copy(t, k, owner):
        peer = lax.rem(li + k, nl)
        return remote(
            reg_own.at[t],
            reg_all.at[t, owner],
            s_ra.at[t, k - 1],
            r_ra.at[t, k - 1],
            "loan",
            peer,
        )

    oht = (pri_row[...] == lax.broadcasted_iota(jnp.int32, (n_reg, owned), 0)).astype(F32)
    eye = (
        lax.broadcasted_iota(jnp.int32, (owned, owned), 0)
        == lax.broadcasted_iota(jnp.int32, (owned, owned), 1)
    ).astype(F32)
    oh = dot(eye.astype(BF16), oht.astype(BF16), NT)
    oh3 = jnp.concatenate([oh, oh, oh], axis=1).astype(BF16)
    oht3 = jnp.concatenate([oht, oht, oht], axis=1).astype(BF16)

    def region_dev(t, u_ref, v_ref):
        for c in range(chains):
            d = PREC * (u_ref[c] - dot(oh3, split3(v_ref[c])))
            dev[c] = d
            reg_part[t, c] = pack(dot(oht3, split3(d)))
        for k in range(1, nl):
            rr_copy(t, k).start()

    def region_reduce(t):
        for k in range(1, nl):
            rr_copy(t, k).wait_recv()
        total = reg_part[t, pl.ds(li * per, per)]
        for k in range(1, nl):
            total = total + reg_buf[t, k - 1]
        reg_own[t] = total
        for k in range(1, nl):
            ra_copy(t, k, li).start()
        reg_all[t, li] = total

    def region_gather(t):
        for k in range(1, nl):
            ra_copy(t, k, lax.rem(li + nl - k, nl)).wait_recv()

    def pool_terms(u_ref):
        for c in range(chains):
            u = u_ref[c]
            hi = u.astype(BF16).astype(F32)
            both = jnp.concatenate([hi, u - hi], axis=1)
            u2[pl.ds(c * owned, owned), :] = both.astype(BF16)

        def chunk(j, carry):
            z = dot(u2[...], slope_t[j])
            m = mask[j]
            for c in range(chains):
                term[j, pl.ds(c, 1), :] = jnp.sum(
                    z[c * owned : (c + 1) * owned] * m, axis=0, keepdims=True
                )
            return carry

        lax.fori_loop(0, nf, chunk, 0)

    def logits(t, b_ref):
        b16 = b_ref[...].astype(BF16)

        def chunk(j, carry):
            part[t, j] = term[j] + dot(b16, rows(j), NT)
            return carry

        lax.fori_loop(0, nf, chunk, 0)
        for k in range(1, nf):
            rs_copy(t, k).start()

    def residuals(t):
        for k in range(1, nf):
            rs_copy(t, k).wait_recv()
        logit = part[t, fi]
        for k in range(1, nf):
            logit = logit + rs_buf[t, k - 1]
        mine = (labels[fi].astype(F32) - jax.nn.sigmoid(logit)).astype(BF16)
        resid[t, fi] = mine
        for k in range(1, nf):
            ag_copy(t, k, fi).start()

    def population(t):
        total = dot(resid[t, fi], rows(fi))
        for k in range(1, nf):
            source = lax.rem(fi + nf - k, nf)
            ag_copy(t, k, source).wait_recv()
            total = total + dot(resid[t, source], rows(source))
        xt_buf[t, 0] = total
        for k in range(1, nl):
            xt_copy(t, k).start()

    def population_sum(t):
        for k in range(1, nl):
            xt_copy(t, k).wait_recv()
        total = xt_buf[t, li]
        for j in range(1, nl):
            total = total + xt_buf[t, lax.rem(li + nl - j, nl)]
        return total

    def likelihood(t):
        resid_f[...] = resid[t].astype(F32)
        lik[...] = jnp.zeros_like(lik)

        def chunk(j, carry):
            m = mask[j]
            a = jnp.concatenate(
                [(resid_f[j, pl.ds(c, 1), :] * m).astype(BF16) for c in range(chains)], axis=0
            )
            lik[...] += dot(a, slope[j])
            return carry

        lax.fori_loop(0, nf, chunk, 0)

    pick_t = (
        lax.broadcasted_iota(jnp.int32, (g_own, feats), 1)
        == stride * lax.broadcasted_iota(jnp.int32, (g_own, feats), 0)
    ).astype(F32).astype(BF16)
    first = li * owned

    def prepare(j, carry):
        x = rows(j)
        st = dot(pick_t, x, NT).astype(BF16)
        slope_t[j] = jnp.concatenate([st, st], axis=0)
        slope[j] = dot(x, pick_t, NT).astype(BF16)
        mask[j] = (
            ids[j] - first == lax.broadcasted_iota(jnp.int32, (owned, width), 0)
        ).astype(F32)
        return carry

    chain = lax.broadcasted_iota(jnp.int32, (chains, 1), 0)
    step_col = jnp.zeros((chains, 1), F32)
    for c in range(chains):
        step_col = jnp.where(chain == c, step_s[c], step_col)
    half = 0.5 * step_col

    pl.semaphore_wait(barrier, nf + nl - 2)
    region_dev(0, pools, regions)
    fetch.wait()
    lax.fori_loop(0, nf, prepare, 0)
    pool_terms(pools)
    logits(0, beta)
    region_reduce(0)
    residuals(0)
    population(0)
    likelihood(0)
    for c in range(chains):
        e = step_s[c]
        m = pool_m[c] + (0.5 * e) * (lik[pl.ds(c * owned, owned), :] - dev[c])
        pool_mn[c] = m
        pools_n[c] = pools[c] + e * m
    region_gather(0)
    for c in range(chains):
        e = step_s[c]
        g = unpack(reg_all[0, c // per, c % per]) - PREC * regions[c]
        m = region_m[c] + (0.5 * e) * g
        region_mn[c] = m
        regions_n[c] = regions[c] + e * m
    region_dev(1, pools_n, regions_n)
    pool_terms(pools_n)
    mb = beta_m[...] + half * (population_sum(0) - total_feats * beta[...])
    beta_mn[...] = mb
    beta_n[...] = beta[...] + step_col * mb
    logits(1, beta_n)
    region_reduce(1)
    residuals(1)
    population(1)
    likelihood(1)
    for c in range(chains):
        pool_mn[c] = pool_mn[c] + (0.5 * step_s[c]) * (lik[pl.ds(c * owned, owned), :] - dev[c])
    region_gather(1)
    for c in range(chains):
        g = unpack(reg_all[1, c // per, c % per]) - PREC * regions_n[c]
        region_mn[c] = region_mn[c] + (0.5 * step_s[c]) * g
    beta_mn[...] = beta_mn[...] + half * (population_sum(1) - total_feats * beta_n[...])
    for t in range(2):
        for k in range(1, nf):
            rs_copy(t, k).wait_send()
            ag_copy(t, k, fi).wait_send()
        for k in range(1, nl):
            xt_copy(t, k).wait_send()
            rr_copy(t, k).wait_send()
            ra_copy(t, k, li).wait_send()


def folds(n_reg, g_own):
    return max(1, min(128 // g_own, n_reg // 8))


def emit(*refs):
    n = len(refs) // 2
    for i in range(n):
        refs[n + i][...] = refs[i][...]


def body(
    nf,
    nl,
    design,
    labels,
    pool_ids,
    pool_region_index,
    step_size,
    beta,
    pools,
    regions,
    beta_momentum,
    pool_momentum,
    region_momentum,
):
    loans, feats = design.shape
    chains, owned, g_own = pools.shape
    n_reg = regions.shape[1]
    width = loans // nf
    fold = folds(n_reg, g_own)
    packed = (n_reg // fold, fold * g_own)
    per = chains // nl
    vmem = pl.BlockSpec(memory_space=pltpu.VMEM)
    smem = pl.BlockSpec(memory_space=pltpu.SMEM)
    hbm = pl.BlockSpec(memory_space=pl.ANY)
    dma = pltpu.SemaphoreType.DMA
    args = (
        design,
        labels.reshape(nf, 1, width),
        pool_ids.reshape(nf, 1, width),
        pool_region_index.reshape(1, owned),
        step_size,
        beta,
        pools,
        regions,
        beta_momentum,
        pool_momentum,
        region_momentum,
    )
    outs = (beta, pools, regions, beta_momentum, pool_momentum, region_momentum)
    shapes = tuple(jax.ShapeDtypeStruct(x.shape, x.dtype) for x in outs)
    results = pl.pallas_call(
        functools.partial(kernel, nf, nl),
        out_shape=shapes,
        in_specs=[{0: hbm, 4: smem}.get(i, vmem) for i in range(len(args))],
        out_specs=tuple(vmem for _ in outs),
        scratch_shapes=[
            pltpu.VMEM((loans, feats), BF16),
            pltpu.VMEM((nf, owned, width), F32),
            pltpu.VMEM((nf, 2 * g_own, width), BF16),
            pltpu.VMEM((nf, width, g_own), BF16),
            pltpu.VMEM((chains * owned, 2 * g_own), BF16),
            pltpu.VMEM((chains, owned, g_own), F32),
            pltpu.VMEM((chains * owned, g_own), F32),
            pltpu.VMEM((nf, chains, width), F32),
            pltpu.VMEM((2, nf, chains, width), F32),
            pltpu.VMEM((2, nf - 1, chains, width), F32),
            pltpu.VMEM((2, nf, chains, width), BF16),
            pltpu.VMEM((nf, chains, width), F32),
            pltpu.VMEM((2, nl, chains, feats), F32),
            pltpu.VMEM((2, chains) + packed, F32),
            pltpu.VMEM((2, nl - 1, per) + packed, F32),
            pltpu.VMEM((2, per) + packed, F32),
            pltpu.VMEM((2, nl, per) + packed, F32),
            dma,
            dma((2, nf - 1)),
            dma((2, nf - 1)),
            dma((2, nf - 1)),
            dma((2, nf - 1)),
            dma((2, nl - 1)),
            dma((2, nl - 1)),
            dma((2, nl - 1)),
            dma((2, nl - 1)),
            dma((2, nl - 1)),
            dma((2, nl - 1)),
        ],
        compiler_params=pltpu.CompilerParams(
            collective_id=0, has_side_effects=True, vmem_limit_bytes=60 << 20
        ),
    )(*args)
    return pl.pallas_call(
        emit,
        out_shape=shapes,
        in_specs=[vmem] * len(shapes),
        out_specs=tuple(vmem for _ in shapes),
    )(*results)


def solution(mesh):
    in_specs = (
        P(("grp", "loan"), "feat"),
        P(("grp", "loan")),
        P(("grp", "loan")),
        P(("grp", "loan")),
        P("grp"),
        P("grp", "feat"),
        P("grp", "loan", "feat"),
        P("grp", None, "feat"),
        P("grp", "feat"),
        P("grp", "loan", "feat"),
        P("grp", None, "feat"),
    )
    out_specs = (
        P("grp", "feat"),
        P("grp", "loan", "feat"),
        P("grp", None, "feat"),
        P("grp", "feat"),
        P("grp", "loan", "feat"),
        P("grp", None, "feat"),
    )
    step = functools.partial(body, mesh.shape["feat"], mesh.shape["loan"])
    return jax.shard_map(step, mesh=mesh, in_specs=in_specs, out_specs=out_specs, check_vma=False)
```
